512 devices in a mesh: width: 8 (over x, core), vocab: 64 (over y, z).
Axes of the slice: x: 4, y: 4, z: 16, core: 2. Of those that a mesh axis runs over, the one named last changes fastest.
Arguments:
- hidden: bfloat16 [1024, 16384], P('vocab', 'width'), may hold values from -6 to 6
- weight: bfloat16 [16384, 65536], P('width', 'vocab'), may hold values from -1 to 1
- policy: bfloat16 [1024, 65536], P('width', 'vocab'), may hold values from -480 to 480
Outputs:
- divergence: float32 [1024], P('width')
- gradient: float32 [1024, 65536], P('width', 'vocab')
The draws below stay inside these ranges and needn't reach their ends.
All inputs are finite; a program needn't handle non-finite values.
Results may differ from the reference program's by a relative error of at most 0.00035.
Values may be sent and summed in bfloat16 or wider, within the bound.
No kernel may reach another device: no remote copies, remote signals or barrier semaphores. Data moves between devices by JAX's collectives and lax.ppermute only.
A program may use at most 64 MiB of HBM per device.

```python
import math
import jax
import jax.numpy as jnp

D = 16384
V = 65536
TOKENS = 1024


def plant_table(key):
    base = jax.random.fold_in(key, 7001)
    directions = jax.random.normal(jax.random.fold_in(base, 1), (3, D), jnp.float32) / math.sqrt(D)
    columns = jnp.arange(3) * (V // 3) + jax.random.randint(jax.random.fold_in(base, 2), (3,), 0, V // 3 - 1)
    spacings = jax.random.uniform(jax.random.fold_in(base, 3), (3,), jnp.float32, 1.0, 3.0)
    strengths = jnp.array([0.35, 0.65, 1.0], jnp.float32)
    return (directions, columns, spacings, strengths)


def draw_weight(key, part):
    noise = jax.random.normal(jax.random.fold_in(key, 11), (D, V), jnp.float32)
    position = jnp.arange(V, dtype=jnp.float32) / V
    scales = 3.0 * jnp.sqrt(1.0 + 0.25 * position) / math.sqrt(D)
    values = noise * scales[None, :]
    directions, columns, spacings, strengths = plant_table(key)
    for planted in range(3):
        values = values.at[:, columns[planted]].set(3.0 * directions[planted])
        lowered = 3.0 - spacings[planted] / (strengths[planted] * math.sqrt(D))
        values = values.at[:, columns[planted] + 1].set(lowered * directions[planted])
    return jnp.clip(values, -1.0, 1.0).astype(jnp.bfloat16)


def draw_hidden(key, part):
    noise = jax.random.normal(jax.random.fold_in(key, 21), (TOKENS, D), jnp.float32)
    values = noise
    return jnp.clip(values, -6.0, 6.0).astype(jnp.bfloat16)


def draw_policy(key, part):
    noise = jnp.clip(jax.random.normal(jax.random.fold_in(key, 31), (TOKENS, V), jnp.float32), -6.0, 6.0)
    position = jnp.arange(V, dtype=jnp.float32) / V
    values = 3.0 * noise + 1.2 * position[None, :]
    return jnp.clip(values, -480.0, 480.0).astype(jnp.bfloat16)


def setup_inputs(seed: int = 0) -> dict:
    key_of = jax.random.split(jax.random.key(seed), 4)
    return {
        "hidden": draw_hidden(jax.random.fold_in(key_of[3], 71), 0),
        "weight": draw_weight(jax.random.fold_in(key_of[3], 71), 0),
        "policy": draw_policy(jax.random.fold_in(key_of[3], 71), 0),
    }


def log_normalize(values):
    largest = jnp.max(values, axis=1, keepdims=True)
    total = jnp.sum(jnp.exp(values - largest), axis=1, keepdims=True)
    return values - (largest + jnp.log(total))


def reference(hidden, weight, policy):
    logits = jnp.dot(hidden, weight, preferred_element_type=jnp.float32)
    log_reference = log_normalize(logits)
    log_policy = log_normalize(policy.astype(jnp.float32))
    log_ratio = log_policy - log_reference
    probability = jnp.exp(log_policy)
    divergence = jnp.sum(probability * log_ratio, axis=1)
    gradient = probability * (log_ratio - divergence[:, None])
    return divergence, gradient
```

```python
import jax
import jax.numpy as jnp
from jax import lax
from jax.sharding import Mesh, PartitionSpec as P

Z = ("zh", "zl")


def spread(value, axes, groups=None):
    size = len(groups[0]) if groups else lax.axis_size(axes)
    return lax.all_to_all(
        jnp.broadcast_to(value[None], (size, *value.shape)), axes, 0, 0, axis_index_groups=groups
    )


def along_z(value, by):
    return lax.ppermute(value, Z, [((i + by) % 16, i) for i in range(16)])


def from_core(value):
    return lax.ppermute(value, "core", [(0, 1), (1, 0)])


def send_x(value, by):
    return lax.ppermute(value, "x", [(i, (i + by) % 4) for i in range(4)])


def product(rows, weight):
    return jnp.dot(rows, weight, preferred_element_type=jnp.float32)


def local_lse(values):
    top = jnp.max(values, axis=1)
    powers = jnp.exp(values - top[:, None])
    return top + jnp.log(jnp.sum(powers, axis=1)), powers


def joint_lse(parts):
    top = jnp.max(parts, axis=0)
    return top + jnp.log(jnp.sum(jnp.exp(parts - top), axis=0))


def body(hidden, weight, policy):
    own_first = [[0, 1, 2, 3], [6, 7, 4, 5]]
    coarse = spread(hidden, ("core", "zh"), own_first)
    first, second = coarse[:, :8], coarse[:, 8:]

    by_owner = [[4 * x + (x + k) % 4 for k in range(4)] for x in range(4)]
    c_own = spread(second, ("x", "y"), by_owner)
    c_own = c_own.reshape(4, 2, 16, 2048).transpose(1, 0, 2, 3).reshape(128, 2048)
    near = [first] + [along_z(first, k) for k in (2, 1, -1)]
    a_own = jnp.stack([near[n] for n in (0, 2, 1, 3)], axis=1).reshape(2, 64, 2048)

    c_plus = along_z(c_own, 1)
    c_minus = along_z(c_own, -1)
    a_all = spread(a_own, ("x", "y"), by_owner)
    c_two_a = along_z(c_own[:64], 2)
    c_two_b = along_z(c_own[64:], -2)

    def chips(parts):
        total = parts[0]
        for k in (2, 1, 3):
            total += send_x(parts[k], k)
        return total


    def early(half):
        return jnp.concatenate([part[half] for part in (c_own, c_plus, c_minus)])

    away = from_core(product(early(slice(64, 128)), weight))
    early = product(early(slice(0, 64)), weight) + away
    early = early.reshape(3, 4, 16, 1024).transpose(1, 0, 2, 3).reshape(4, 48, 1024)
    early = chips(early)

    c_away = from_core(product(c_two_b, weight))
    a_send = product(a_all[:, 1].reshape(256, 2048), weight)
    a_away = from_core(a_send)
    c_late = (product(c_two_a, weight) + c_away).reshape(4, 16, 1024)
    a_late = (product(a_all[:, 0].reshape(256, 2048), weight) + a_away).reshape(4, 64, 1024)
    late = chips(jnp.concatenate([c_late, a_late], axis=1))

    c_logits = [early[:16], early[16:32], late[:16], early[32:]]
    c_logits = jnp.stack([part.reshape(2, 8, 1024) for part in c_logits], axis=1)
    a_logits = late[16:].reshape(2, 4, 8, 1024)
    logits = jnp.stack([a_logits, c_logits], axis=2)
    logits = jnp.roll(logits, lax.axis_index("zl"), axis=1).reshape(128, 1024)

    values = policy.astype(jnp.float32)
    policy_lse, powers = local_lse(values)
    difference = values - logits
    mean = jnp.sum(powers * difference, axis=1) / jnp.sum(powers, axis=1)
    parts = jnp.stack([local_lse(logits)[0], policy_lse, mean])
    parts = spread(parts, ("y", "zh", "zl"))
    reference_lse = joint_lse(parts[:, 0])
    policy_lse = joint_lse(parts[:, 1])
    mean = jnp.sum(jnp.exp(parts[:, 1] - policy_lse) * parts[:, 2], axis=0)
    divergence = mean - policy_lse + reference_lse
    gradient = jnp.exp(values - policy_lse[:, None]) * (difference - mean[:, None])
    return (divergence, gradient)


def solution(mesh):
    split = Mesh(mesh.devices.reshape(4, 2, 4, 4, 4), ("x", "core", "y", "zh", "zl"))
    rows, columns = ("y", "zh", "zl"), ("x", "core")

    def step(*args):
        return body(*args)

    step = jax.shard_map(
        step,
        mesh=split,
        in_specs=(P(rows, columns), P(columns, rows), P(columns, rows)),
        out_specs=(P(columns), P(columns, rows)),
        check_vma=False,
    )
    return step
```

```python
import jax
import jax.numpy as jnp
from jax import lax
from jax.sharding import Mesh, PartitionSpec as P

Z = ("zh", "zl")


def spread(value, axes, groups=None):
    size = len(groups[0]) if groups else lax.axis_size(axes)
    return lax.all_to_all(
        jnp.broadcast_to(value[None], (size, *value.shape)), axes, 0, 0, axis_index_groups=groups
    )


def along_z(value, by):
    return lax.ppermute(value, Z, [((i + by) % 16, i) for i in range(16)])


def from_core(value):
    return lax.ppermute(value, "core", [(0, 1), (1, 0)])


def send_x(value, by):
    return lax.ppermute(value, "x", [(i, (i + by) % 4) for i in range(4)])


def product(rows, weight):
    return jnp.dot(rows, weight, preferred_element_type=jnp.float32)


def local_lse(values):
    top = jnp.max(values, axis=1)
    powers = jnp.exp(values - top[:, None])
    return top + jnp.log(jnp.sum(powers, axis=1)), powers


def joint_lse(parts):
    top = jnp.max(parts, axis=0)
    return top + jnp.log(jnp.sum(jnp.exp(parts - top), axis=0))


def body(hidden, weight, policy):
    own_first = [[0, 1, 2, 3], [6, 7, 4, 5]]
    coarse = spread(hidden, ("core", "zh"), own_first)
    first, second = coarse[:, :8], coarse[:, 8:]

    by_owner = [[4 * x + (x + k) % 4 for k in range(4)] for x in range(4)]
    c_own = spread(second, ("x", "y"), by_owner)
    c_own = c_own.reshape(4, 2, 16, 2048).transpose(1, 0, 2, 3).reshape(128, 2048)
    near = [first] + [along_z(first, k) for k in (2, 1, -1)]
    a_own = jnp.stack([near[n] for n in (0, 2, 1, 3)], axis=1).reshape(2, 64, 2048)

    c_plus = along_z(c_own, 1)
    c_minus = along_z(c_own, -1)
    a_all = spread(a_own, ("x", "y"), by_owner)
    c_two_a = along_z(c_own[:64], 2)
    c_two_b = along_z(c_own[64:], -2)

    def chips(parts):
        total = parts[0]
        for k in (2, 1, 3):
            total += send_x(parts[k], k)
        return total

    def early(half):
        return product(jnp.concatenate([part[half] for part in (c_own, c_plus, c_minus)]), weight)

    away = from_core(early(slice(64, 128)))
    early = (early(slice(0, 64)) + away).reshape(3, 4, 16, 1024)

    def late(c_rows, a_rows):
        rows = jnp.concatenate([c_rows.reshape(4, 16, 2048), a_rows], axis=1)
        return product(rows.reshape(320, 2048), weight)

    away = from_core(late(c_two_b, a_all[:, 1]))
    late = (late(c_two_a, a_all[:, 0]) + away).reshape(4, 80, 1024)
    sums = [jnp.concatenate([*early[:, k], late[k]]) for k in range(4)]
    sums = chips(sums)

    c_logits = [sums[:16], sums[16:32], sums[48:64], sums[32:48]]
    c_logits = jnp.stack([part.reshape(2, 8, 1024) for part in c_logits], axis=1)
    a_logits = sums[64:].reshape(2, 4, 8, 1024)
    logits = jnp.stack([a_logits, c_logits], axis=2)
    logits = jnp.roll(logits, lax.axis_index("zl"), axis=1).reshape(128, 1024)

    values = policy.astype(jnp.float32)
    policy_lse, powers = local_lse(values)
    difference = values - logits
    mean = jnp.sum(powers * difference, axis=1) / jnp.sum(powers, axis=1)
    parts = jnp.stack([local_lse(logits)[0], policy_lse, mean])
    parts = spread(parts, ("y", "zh", "zl"))
    reference_lse = joint_lse(parts[:, 0])
    policy_lse = joint_lse(parts[:, 1])
    mean = jnp.sum(jnp.exp(parts[:, 1] - policy_lse) * parts[:, 2], axis=0)
    divergence = mean - policy_lse + reference_lse
    gradient = jnp.exp(values - policy_lse[:, None]) * (difference - mean[:, None])
    return (divergence, gradient)


def solution(mesh):
    split = Mesh(mesh.devices.reshape(4, 2, 4, 4, 4), ("x", "core", "y", "zh", "zl"))
    rows, columns = ("y", "zh", "zl"), ("x", "core")

    def step(*args):
        return body(*args)

    step = jax.shard_map(
        step,
        mesh=split,
        in_specs=(P(rows, columns), P(columns, rows), P(columns, rows)),
        out_specs=(P(columns), P(columns, rows)),
        check_vma=False,
    )
    return step
```

```python
import jax
import jax.numpy as jnp
from jax import lax
from jax.sharding import Mesh, PartitionSpec as P

Z = ("zh", "zl")


def spread(value, axes, groups=None):
    size = len(groups[0]) if groups else lax.axis_size(axes)
    return lax.all_to_all(
        jnp.broadcast_to(value[None], (size, *value.shape)), axes, 0, 0, axis_index_groups=groups
    )


def along_z(value, by):
    return lax.ppermute(value, Z, [((i + by) % 16, i) for i in range(16)])


def from_core(value):
    return lax.ppermute(value, "core", [(0, 1), (1, 0)])


def send_x(value, by):
    return lax.ppermute(value, "x", [(i, (i + by) % 4) for i in range(4)])


def product(rows, weight):
    return jnp.dot(rows, weight, preferred_element_type=jnp.float32)


def local_lse(values):
    top = jnp.max(values, axis=1)
    powers = jnp.exp(values - top[:, None])
    return top + jnp.log(jnp.sum(powers, axis=1)), powers


def joint_lse(parts):
    top = jnp.max(parts, axis=0)
    return top + jnp.log(jnp.sum(jnp.exp(parts - top), axis=0))


def body(hidden, weight, policy):
    own_first = [[0, 1, 2, 3], [6, 7, 4, 5]]
    coarse = spread(hidden, ("core", "zh"), own_first)
    first, second = coarse[:, :8], coarse[:, 8:]

    by_owner = [[4 * x + (x + k) % 4 for k in range(4)] for x in range(4)]
    c_own = spread(second, ("x", "y"), by_owner)
    c_own = c_own.reshape(4, 2, 16, 2048).transpose(1, 0, 2, 3).reshape(128, 2048)
    near = [first] + [along_z(first, k) for k in (2, 1, -1)]
    a_own = jnp.stack([near[n] for n in (0, 2, 1, 3)], axis=1).reshape(2, 64, 2048)

    c_plus = along_z(c_own, 1)
    c_minus = along_z(c_own, -1)
    a_all = spread(a_own, ("x", "y"), by_owner)
    halves = c_own[:64], c_own[64:]
    c_two_a = along_z(halves[0], 2)
    c_two_b = along_z(halves[1], -2)

    def chips(parts):
        total = parts[0]
        for k in (2, 1, 3):
            total += send_x(parts[k], k)
        return total

    early = [product(part, weight) for part in (c_own, c_plus, c_minus)]
    early_away = jnp.concatenate([part[64:] for part in early])
    early_away = from_core(early_away).reshape(3, 4, 16, 1024)

    def late(c_rows, a_rows):
        rows = jnp.concatenate([c_rows.reshape(4, 16, 2048), a_rows], axis=1)
        return product(rows.reshape(320, 2048), weight)

    late_away = from_core(late(c_two_b, a_all[:, 1]))
    late_away = late_away.reshape(4, 80, 1024)
    late_kept = lax.optimization_barrier(late(c_two_a, a_all[:, 0]))
    sums = []
    for k in range(4):
        own = [part[16 * k : 16 * k + 16] for part in early]
        own = jnp.concatenate([*own, late_kept[80 * k : 80 * k + 80]])
        sums.append(own + jnp.concatenate([*early_away[:, k], late_away[k]]))
    sums = chips(sums)

    c_logits = [sums[:16], sums[16:32], sums[48:64], sums[32:48]]
    c_logits = jnp.stack([part.reshape(2, 8, 1024) for part in c_logits], axis=1)
    a_logits = sums[64:].reshape(2, 4, 8, 1024)
    logits = jnp.stack([a_logits, c_logits], axis=2)
    logits = jnp.roll(logits, lax.axis_index("zl"), axis=1).reshape(128, 1024)

    values = policy.astype(jnp.float32)
    policy_lse, powers = local_lse(values)
    difference = values - logits
    mean = jnp.sum(powers * difference, axis=1) / jnp.sum(powers, axis=1)
    parts = jnp.stack([local_lse(logits)[0], policy_lse, mean])
    parts = spread(parts, ("y", "zh", "zl"))
    reference_lse = joint_lse(parts[:, 0])
    policy_lse = joint_lse(parts[:, 1])
    mean = jnp.sum(jnp.exp(parts[:, 1] - policy_lse) * parts[:, 2], axis=0)
    divergence = mean - policy_lse + reference_lse
    gradient = jnp.exp(values - policy_lse[:, None]) * (difference - mean[:, None])
    return (divergence, gradient)


def solution(mesh):
    split = Mesh(mesh.devices.reshape(4, 2, 4, 4, 4), ("x", "core", "y", "zh", "zl"))
    rows, columns = ("y", "zh", "zl"), ("x", "core")

    def step(*args):
        return body(*args)

    step = jax.shard_map(
        step,
        mesh=split,
        in_specs=(P(rows, columns), P(columns, rows), P(columns, rows)),
        out_specs=(P(columns), P(columns, rows)),
        check_vma=False,
    )
    return step
```

```python
import jax
import jax.numpy as jnp
from jax import lax
from jax.sharding import Mesh, PartitionSpec as P

Z = ("zh", "zl")


def spread(value, axes, groups=None):
    size = len(groups[0]) if groups else lax.axis_size(axes)
    return lax.all_to_all(
        jnp.broadcast_to(value[None], (size, *value.shape)), axes, 0, 0, axis_index_groups=groups
    )


def along_z(value, by):
    return lax.ppermute(value, Z, [((i + by) % 16, i) for i in range(16)])


def across_z(value):
    return lax.ppermute(value, Z, [(i, (i + 2 - 4 * (i % 2)) % 16) for i in range(16)])


def from_core(value):
    return lax.ppermute(value, "core", [(0, 1), (1, 0)])


def send_x(value, by):
    return lax.ppermute(value, "x", [(i, (i + by) % 4) for i in range(4)])


def product(rows, weight):
    return jnp.dot(rows, weight, preferred_element_type=jnp.float32)


def local_lse(values):
    top = jnp.max(values, axis=1)
    powers = jnp.exp(values - top[:, None])
    return top + jnp.log(jnp.sum(powers, axis=1)), powers


def joint_lse(parts):
    top = jnp.max(parts, axis=0)
    return top + jnp.log(jnp.sum(jnp.exp(parts - top), axis=0))


def body(hidden, weight, policy):
    own_first = [[0, 1, 2, 3], [6, 7, 4, 5]]
    coarse = spread(hidden, ("core", "zh"), own_first)
    first, second = coarse[:, :8], coarse[:, 8:]

    by_owner = [[4 * x + (x + k) % 4 for k in range(4)] for x in range(4)]
    c_own = spread(second, ("x", "y"), by_owner)
    c_own = c_own.reshape(4, 2, 16, 2048).transpose(1, 0, 2, 3).reshape(128, 2048)
    near = [first, across_z(first)]
    near += [along_z(first, k) for k in (1, -1)]
    a_own = jnp.stack([near[n] for n in (0, 2, 1, 3)], axis=1).reshape(2, 64, 2048)

    c_plus = along_z(c_own, 1)
    c_minus = along_z(c_own, -1)
    a_all = spread(a_own, ("x", "y"), by_owner)
    c_two = across_z(c_own)

    def chips(parts):
        total = parts[0]
        for k in (2, 1, 3):
            total += send_x(parts[k], k)
        return total

    early = [product(part, weight) for part in (c_own, c_plus, c_minus)]
    early_away = jnp.concatenate([part[64:].reshape(4, 16, 1024) for part in early], axis=1)
    early_away = from_core(early_away.reshape(192, 1024))

    def late(c_rows, a_rows):
        rows = jnp.concatenate([c_rows.reshape(4, 16, 2048), a_rows], axis=1)
        return product(rows.reshape(320, 2048), weight)

    late_away = from_core(late(c_two[64:], a_all[:, 1]))
    late_kept = lax.optimization_barrier(late(c_two[:64], a_all[:, 0]))
    sums = []
    for k in range(4):
        own = [part[16 * k : 16 * k + 16] for part in early]
        own = jnp.concatenate([*own, late_kept[80 * k : 80 * k + 80]])
        away = [early_away[48 * k : 48 * k + 48], late_away[80 * k : 80 * k + 80]]
        sums.append(own + jnp.concatenate(away))
    sums = chips(sums)

    c_logits = [sums[:16], sums[16:32], sums[48:64], sums[32:48]]
    c_logits = jnp.stack([part.reshape(2, 8, 1024) for part in c_logits], axis=1)
    a_logits = sums[64:].reshape(2, 4, 8, 1024)
    logits = jnp.stack([a_logits, c_logits], axis=2)
    logits = jnp.roll(logits, lax.axis_index("zl"), axis=1).reshape(128, 1024)

    values = policy.astype(jnp.float32)
    policy_lse, powers = local_lse(values)
    difference = values - logits
    mean = jnp.sum(powers * difference, axis=1) / jnp.sum(powers, axis=1)
    parts = jnp.stack([local_lse(logits)[0], policy_lse, mean])
    parts = spread(parts, ("y", "zh", "zl"))
    reference_lse = joint_lse(parts[:, 0])
    policy_lse = joint_lse(parts[:, 1])
    mean = jnp.sum(jnp.exp(parts[:, 1] - policy_lse) * parts[:, 2], axis=0)
    divergence = mean - policy_lse + reference_lse
    gradient = jnp.exp(values - policy_lse[:, None]) * (difference - mean[:, None])
    return (divergence, gradient)


def solution(mesh):
    split = Mesh(mesh.devices.reshape(4, 2, 4, 4, 4), ("x", "core", "y", "zh", "zl"))
    rows, columns = ("y", "zh", "zl"), ("x", "core")

    def step(*args):
        return body(*args)

    step = jax.shard_map(
        step,
        mesh=split,
        in_specs=(P(rows, columns), P(columns, rows), P(columns, rows)),
        out_specs=(P(columns), P(columns, rows)),
        check_vma=False,
    )
    return step
```

```python
import jax
import jax.numpy as jnp
from jax import lax
from jax.sharding import Mesh, PartitionSpec as P

Z = ("zh", "zl")


def spread(value, axes, groups=None):
    size = len(groups[0]) if groups else lax.axis_size(axes)
    return lax.all_to_all(
        jnp.broadcast_to(value[None], (size, *value.shape)), axes, 0, 0, axis_index_groups=groups
    )


def along_z(value, by):
    return lax.ppermute(value, Z, [((i + by) % 16, i) for i in range(16)])


def across_z(value):
    return lax.ppermute(value, Z, [(i, (i + 2 - 4 * (i % 2)) % 16) for i in range(16)])


def from_core(value):
    return lax.ppermute(value, "core", [(0, 1), (1, 0)])


def send_x(value, by):
    return lax.ppermute(value, "x", [(i, (i + by) % 4) for i in range(4)])


def product(rows, weight):
    return jnp.dot(rows, weight, preferred_element_type=jnp.float32)


def local_lse(values):
    top = jnp.max(values, axis=1)
    powers = jnp.exp(values - top[:, None])
    return top + jnp.log(jnp.sum(powers, axis=1)), powers


def joint_lse(parts):
    top = jnp.max(parts, axis=0)
    return top + jnp.log(jnp.sum(jnp.exp(parts - top), axis=0))


def body(hidden, weight, policy):
    own_first = [[0, 1, 2, 3], [6, 7, 4, 5]]
    coarse = spread(hidden, ("core", "zh"), own_first)
    first, second = coarse[:, :8], coarse[:, 8:]

    by_owner = [[4 * x + (x + k) % 4 for k in range(4)] for x in range(4)]
    c_own = spread(second, ("x", "y"), by_owner)
    c_own = c_own.reshape(4, 2, 16, 2048).transpose(1, 0, 2, 3).reshape(128, 2048)
    near = [first, across_z(first)]
    near += [along_z(first, k) for k in (1, -1)]
    a_own = jnp.stack([near[n] for n in (0, 2, 1, 3)], axis=1).reshape(2, 64, 2048)

    c_plus = along_z(c_own, 1)
    c_minus = along_z(c_own, -1)
    a_all = spread(a_own, ("x", "y"), by_owner)
    c_two = across_z(c_own)

    def chips(parts):
        total = parts[0]
        for k in (2, 1, 3):
            total += send_x(parts[k], k)
        return total

    early = [product(part, weight) for part in (c_own, c_plus)]
    early_away = jnp.concatenate([part[64:].reshape(4, 16, 1024) for part in early], axis=1)
    early_away = from_core(early_away.reshape(128, 1024))

    def late(side):
        rows = [part.reshape(2, 4, 16, 2048)[side] for part in (c_minus, c_two)]
        rows = jnp.concatenate([*rows, a_all[:, side]], axis=1)
        return product(rows.reshape(384, 2048), weight)

    late_away = from_core(late(1))
    late_kept = lax.optimization_barrier(late(0))
    sums = []
    for k in range(4):
        own = [part[16 * k : 16 * k + 16] for part in early]
        own = jnp.concatenate([*own, late_kept[96 * k : 96 * k + 96]])
        away = [early_away[32 * k : 32 * k + 32], late_away[96 * k : 96 * k + 96]]
        sums.append(own + jnp.concatenate(away))
    sums = chips(sums)

    c_logits = [sums[:16], sums[16:32], sums[48:64], sums[32:48]]
    c_logits = jnp.stack([part.reshape(2, 8, 1024) for part in c_logits], axis=1)
    a_logits = sums[64:].reshape(2, 4, 8, 1024)
    logits = jnp.stack([a_logits, c_logits], axis=2)
    logits = jnp.roll(logits, lax.axis_index("zl"), axis=1).reshape(128, 1024)

    values = policy.astype(jnp.float32)
    policy_lse, powers = local_lse(values)
    difference = values - logits
    mean = jnp.sum(powers * difference, axis=1) / jnp.sum(powers, axis=1)
    parts = jnp.stack([local_lse(logits)[0], policy_lse, mean])
    parts = spread(parts, ("y", "zh", "zl"))
    reference_lse = joint_lse(parts[:, 0])
    policy_lse = joint_lse(parts[:, 1])
    mean = jnp.sum(jnp.exp(parts[:, 1] - policy_lse) * parts[:, 2], axis=0)
    divergence = mean - policy_lse + reference_lse
    gradient = jnp.exp(values - policy_lse[:, None]) * (difference - mean[:, None])
    return (divergence, gradient)


def solution(mesh):
    split = Mesh(mesh.devices.reshape(4, 2, 4, 4, 4), ("x", "core", "y", "zh", "zl"))
    rows, columns = ("y", "zh", "zl"), ("x", "core")

    def step(*args):
        return body(*args)

    step = jax.shard_map(
        step,
        mesh=split,
        in_specs=(P(rows, columns), P(columns, rows), P(columns, rows)),
        out_specs=(P(columns), P(columns, rows)),
        check_vma=False,
    )
    return step
```
